256 devices in a mesh: row: 16 (over y, x), col: 8 (over z_lo, core), band: 2 (over z_hi).
Axes of the slice: x: 4, y: 4, z: 8 (z_hi: 2, z_lo: 4; z = z_hi * 4 + z_lo), core: 2. Of those that a mesh axis runs over, the one named last changes fastest.
Arguments:
- panel: bfloat16 [32, 512, 512], P('row', ('col', 'band')), may hold values from -6 to 6
- inverse: bfloat16 [2, 512, 512], replicated, may hold values from -0.25 to 0.25
- trail_grad: bfloat16 [32, 32, 512, 512], P('row', ('col', 'band')), may hold values from -0.046875 to 0.046875
- factor_grad: bfloat16 [32, 512, 512], P('row', ('col', 'band')), may hold values from -6 to 6
- present: int32 [32, 32], P('row', ('col', 'band')), may hold values from 0 to 1, as said below
- supernode: int32 [32], replicated, may hold values from 0 to 1
Outputs:
- panel_adjoint: bfloat16 [32, 512, 512], P('row', ('col', 'band'))
- inverse_adjoint: float32 [2, 512, 512], replicated
The draws below stay inside these ranges and needn't reach their ends.
Inputs may be any that keep to these rules, and one draw needn't show every extreme that they name: Every diagonal tile is present; rows differ widely in how many tiles are present.
All inputs are finite; a program needn't handle non-finite values.
Results may differ from the reference program's by a relative error of at most 0.0055.
Values may be sent and summed in bfloat16 or wider, within the bound.
A program may use at most 64 MiB of HBM per device.

```python
import jax
import jax.numpy as jnp
from jax import lax

TILE = 512
NT = 32


def draw_present(key, part):
    key_rows = jax.random.fold_in(key, 11)
    key_cells = jax.random.fold_in(key, 12)
    limits = jax.random.randint(key_rows, (NT, 1), 1, 17)
    cells = jax.random.randint(key_cells, (NT, NT), 0, 16)
    flags = (cells < limits).astype(jnp.int32)
    rows = jnp.arange(NT, dtype=jnp.int32)
    return jnp.where(rows[:, None] == rows[None, :], 1, flags).astype(jnp.int32)


def draw_supernode(key, part):
    return jax.random.randint(jax.random.fold_in(key, 21), (NT,), 0, 2).astype(jnp.int32)


def spiked(result, stream_key, source, target, blocks, factor):
    def block_of(axis_at):
        return (jnp.arange(result.shape[axis_at]) // (result.shape[axis_at] // blocks)).reshape((-1,) + (1,) * (result.ndim - 1 - axis_at))

    first = jax.random.permutation(stream_key, blocks)[block_of(target)]
    far = (block_of(target) + blocks // 2) % blocks
    return jnp.where((block_of(source) == first) | (block_of(source) == far), factor * result, result)


def levels(key, extent, shards, low, largest):
    def one(axis_at, blocks):
        steps = jax.random.uniform(jax.random.fold_in(jax.random.fold_in(key, 6), axis_at), (blocks,), jnp.float32, low / len(shards), largest / len(shards))
        return jnp.repeat(jnp.exp(steps), extent[axis_at] // blocks).reshape((-1,) + (1,) * (len(extent) - axis_at - 1))

    gain = one(*shards[0])
    for cut in shards[1:]:
        gain = gain * one(*cut)
    return gain


def noise(rng, extent, width, bound, cuts=(), kind=jnp.bfloat16):
    values = width * jax.random.normal(rng, extent, jnp.float32)
    if cuts:
        values = values * levels(rng, extent, cuts, -0.22, 0.18)
    return jnp.clip(values, -bound, bound).astype(kind)


def noise_with(own_key, shape, scale, most, split, heavy, held_as=jnp.bfloat16):
    drawn = scale * jax.random.normal(own_key, shape, jnp.float32)
    if split:
        drawn = drawn * levels(own_key, shape, split, -0.22, 0.18)
    return jnp.clip(spiked(drawn, jax.random.fold_in(own_key, 3), *heavy), -most, most).astype(held_as)


def setup_inputs(seed: int = 0) -> dict:
    splits = jax.random.split(jax.random.key(seed), 7)
    panel = noise(splits[0], (NT, TILE, TILE), 1.0, 6.0, ((0, 16), (1, 16)))
    inverse = noise(splits[1], (2, TILE, TILE), TILE ** -0.5, 0.25)
    trail_grad = noise_with(splits[2], (NT, NT, TILE, TILE), (1.0 / (NT * TILE) ** 0.5), 0.046875, ((0, 16), (1, 16)), (1, 2, 16, 2.0))
    factor_grad = noise(splits[3], (NT, TILE, TILE), 1.0, 6.0, ((0, 16), (1, 16)))
    present = draw_present(jax.random.fold_in(splits[6], 71), 0)
    supernode = draw_supernode(jax.random.fold_in(splits[6], 71), 0)
    return {"panel": panel, "inverse": inverse, "trail_grad": trail_grad, "factor_grad": factor_grad, "present": present, "supernode": supernode}


def reference(panel, inverse, trail_grad, factor_grad, present, supernode):
    chosen = inverse[supernode].astype(jnp.float32)
    factor = jnp.einsum('iab,ibc->iac', panel.astype(jnp.float32), chosen).astype(jnp.bfloat16)
    weight = present * (supernode[:, None] == supernode[None, :]).astype(jnp.int32)
    factor_wide = factor.astype(jnp.float32)

    def direct_row(index):
        tiles = trail_grad[index].astype(jnp.float32) * weight[index].astype(jnp.float32)[:, None, None]
        return jnp.einsum('jab,jbe->ae', tiles, factor_wide)

    def mirror_col(index):
        tiles = trail_grad[:, index].astype(jnp.float32) * weight[:, index].astype(jnp.float32)[:, None, None]
        return jnp.einsum('iab,iae->be', tiles, factor_wide)
    indices = jnp.arange(NT, dtype=jnp.int32)
    direct = lax.map(direct_row, indices)
    mirror = lax.map(mirror_col, indices)
    factor_total = (factor_grad.astype(jnp.float32) - direct - mirror).astype(jnp.bfloat16)
    panel_adjoint = jnp.einsum('iae,ife->iaf', factor_total.astype(jnp.float32), chosen).astype(jnp.bfloat16)
    onehot = (supernode[:, None] == jnp.arange(2, dtype=jnp.int32)[None, :]).astype(jnp.float32)
    terms = jnp.einsum('iaf,iae->ife', panel.astype(jnp.float32), factor_total.astype(jnp.float32))
    inverse_adjoint = jnp.einsum('is,ife->sfe', onehot, terms) / jnp.sqrt(jnp.float32(NT * TILE))
    return (panel_adjoint, inverse_adjoint)
```

```python
import jax
import jax.numpy as jnp
from jax import lax
from jax.experimental import pallas as pl
from jax.experimental.pallas import tpu as pltpu
from jax.sharding import PartitionSpec as P

MESH = pl.DeviceIdType.MESH
F32 = jnp.float32
BF16 = jnp.bfloat16
N = 16
ZN = 8
R = 32
TILE = 512


def rem(a, b):
    return lax.rem(a, jnp.int32(b))


def div(a, b):
    return lax.div(a, jnp.int32(b))


def loop(lo, hi, body):
    def step(i, carry):
        body(i)
        return carry

    lax.fori_loop(lo, hi, step, 0)


def kernel(
    panel, inverse, trail_hbm, factor_grad, present, supernode,
    adjoint, inv_out,
    tm, tt, frow, pg, fcol, dpart, dsib, dsum, drecv, dtot, mpart, mrecv, mred, mfin,
    tslice, trecv, rpart, rrecv, gz, gx,
    t_sem, fz_s, fz_r, pz_s, pz_r, perm_s, perm_r, fx_s, fx_r,
    ds_s, ds_r, dz_s, dz_r, mx_s, mx_r, mp_s, mp_r, tz_s, tz_r, rx_s, rx_r, gz_s, gz_r, gx_s, gx_r,
):
    r = lax.axis_index("row")
    col = lax.axis_index("col")
    band = lax.axis_index("band")
    core = rem(col, 2)
    z = band * 4 + div(col, 2)
    c = col * 2 + band
    sib_col = col + 1 - 2 * core

    def z_dev(k):
        return (r, div(k, 2), rem(k, 2))

    def x_dev(p):
        return (p, col, band)

    def index_at(zz, cc):
        return rem(zz, 4) * 4 + cc * 2 + div(zz, 4)

    def ring(d):
        half = div(d + 1, 2)
        return rem(z + ZN + half * (2 * rem(d, 2) - 1), ZN)

    sib = (r, sib_col, band)
    turned = (c, div(r, 2), rem(r, 2))

    def remote(src, dst, ss, rs, dev):
        return pltpu.make_async_remote_copy(
            src_ref=src, dst_ref=dst, send_sem=ss, recv_sem=rs, device_id=dev, device_id_type=MESH
        )

    trail_copy = pltpu.make_async_copy(trail_hbm, tm, t_sem)
    trail_copy.start()

    barrier = pltpu.get_barrier_semaphore()

    def greet(d):
        pl.semaphore_signal(barrier, inc=1, device_id=z_dev(rem(c + d, N)), device_id_type=MESH)
        pl.semaphore_signal(barrier, inc=1, device_id=x_dev(rem(r + d, N)), device_id_type=MESH)

    loop(1, N, greet)

    @pl.when(r != c)
    def _():
        pl.semaphore_signal(barrier, inc=1, device_id=turned, device_id_type=MESH)

    s_row = [supernode[2 * r + i] for i in range(2)]
    s_col = [supernode[2 * c + j] for j in range(2)]

    mine = panel[...].reshape(2 * R, TILE)
    y0 = jnp.dot(mine, inverse[0], preferred_element_type=F32)
    y1 = jnp.dot(mine, inverse[1], preferred_element_type=F32)
    row_tile = lax.broadcasted_iota(jnp.int32, (2 * R, TILE), 0) // R
    row_super = jnp.where(row_tile == 0, s_row[0], s_row[1])
    piece = jnp.where(row_super == 0, y0, y1).astype(BF16)
    frow[c] = piece
    pg[c] = mine

    @pl.when(r == c)
    def _():
        fcol[r] = piece

    @pl.when(r == c)
    def _():
        pl.semaphore_wait(barrier, 2 * (N - 1))

    @pl.when(r != c)
    def _():
        pl.semaphore_wait(barrier, 2 * (N - 1) + 1)
        remote(frow.at[c], fcol.at[c], perm_s, perm_r, turned).start()

    def gather_z_start(buf, ss, rs):
        def send(d):
            k = index_at(ring(d), core)
            remote(buf.at[c], buf.at[c], ss.at[d], rs.at[c], z_dev(k)).start()

        loop(1, ZN, send)
        remote(buf.at[c], buf.at[c], ss.at[0], rs.at[c], sib).start()

    def gather_z_pass(buf, ss, rs):
        def forward(d):
            k = index_at(ring(d), core)
            copy = remote(buf.at[k], buf.at[k], ss.at[ZN - 1 + d], rs.at[k], sib)
            copy.wait_recv()
            copy.start()

        loop(1, ZN, forward)

    def gather_z_end(buf, ss, rs):
        def finish(d):
            k = index_at(rem(z + d, ZN), 1 - core)
            remote(buf.at[k], buf.at[k], ss.at[d], rs.at[k], sib).wait_recv()

        loop(0, ZN, finish)

        def drain(d):
            remote(buf.at[c], buf.at[c], ss.at[d], rs.at[c], sib).wait_send()

        loop(0, 2 * ZN - 1, drain)

    gather_z_start(frow, fz_s, fz_r)
    gather_z_start(pg, pz_s, pz_r)

    trail_copy.wait()
    for i in range(2):
        for j in range(2):
            weight = present[i, j] * (s_row[i] == s_col[j]).astype(jnp.int32)
            kept = tm[i, j].astype(F32) * weight.astype(F32)
            tm[i, j] = kept.astype(BF16)
            tt[i, j] = kept.T.astype(BF16)

    @pl.when(r != c)
    def _():
        remote(frow.at[c], fcol.at[r], perm_s, perm_r, turned).wait_recv()

    def gather_x(d):
        remote(fcol.at[r], fcol.at[r], fx_s.at[d], fx_r.at[r], x_dev(rem(r + d, N))).start()

    loop(1, N, gather_x)

    gather_z_pass(frow, fz_s, fz_r)
    gather_z_end(frow, fz_s, fz_r)

    for j in range(2):
        total = jnp.zeros((TILE, TILE), F32)
        for i in range(2):
            rows = frow[:, i * R:(i + 1) * R, :].reshape(TILE, TILE)
            total = total + jnp.dot(tt[i, j], rows, preferred_element_type=F32)
        mpart[:, j * R:(j + 1) * R, :] = total.astype(BF16).reshape(N, R, TILE)

    def scatter_x(d):
        p = rem(r + d, N)
        remote(mpart.at[p], mrecv.at[r], mx_s.at[d], mx_r.at[r], x_dev(p)).start()

    loop(1, N, scatter_x)

    gather_z_pass(pg, pz_s, pz_r)

    def wait_x(d):
        p = rem(r + d, N)
        remote(fcol.at[p], fcol.at[p], fx_s.at[d], fx_r.at[p], x_dev(p)).wait_recv()

    loop(1, N, wait_x)

    for i in range(2):
        total = jnp.zeros((TILE, TILE), F32)
        for j in range(2):
            rows = fcol[:, j * R:(j + 1) * R, :].reshape(TILE, TILE)
            total = total + jnp.dot(tm[i, j], rows, preferred_element_type=F32)
        dpart[:, i * R:(i + 1) * R, :] = total.astype(BF16).reshape(N, R, TILE)

    def to_sibling(d):
        k = index_at(ring(ZN - 1 - d), 1 - core)
        remote(dpart.at[k], dsib.at[k], ds_s.at[d], ds_r.at[k], sib).start()

    loop(0, ZN, to_sibling)

    def pair_sum(d):
        k = index_at(ring(ZN - 1 - d), core)
        remote(dsib.at[k], dsib.at[k], ds_s.at[d], ds_r.at[k], sib).wait_recv()
        dsum[k] = (dpart[k].astype(F32) + dsib[k].astype(F32)).astype(BF16)
        remote(dsum.at[k], drecv.at[c], dz_s.at[d], dz_r.at[c], z_dev(k)).start()

    loop(0, ZN - 1, pair_sum)
    remote(dsib.at[c], dsib.at[c], ds_s.at[0], ds_r.at[c], sib).wait_recv()
    dtot[...] = dpart[c].astype(F32) + dsib[c].astype(F32)

    mred[...] = mpart[r].astype(F32)

    def mirror_sum(d):
        p = rem(r + d, N)
        remote(mrecv.at[p], mrecv.at[p], mx_s.at[d], mx_r.at[p], x_dev(p)).wait_recv()
        mred[...] = mred[...] + mrecv[p].astype(F32)

    loop(1, N, mirror_sum)
    mfin[0] = mred[...].astype(BF16)

    @pl.when(r == c)
    def _():
        mfin[1] = mred[...].astype(BF16)

    @pl.when(r != c)
    def _():
        remote(mfin.at[0], mfin.at[1], mp_s, mp_r, turned).start()

    def direct_sum(d):
        k = index_at(ring(d), core)
        remote(drecv.at[k], drecv.at[k], dz_s.at[d], dz_r.at[k], z_dev(k)).wait_recv()
        dtot[...] = dtot[...] + drecv[k].astype(F32)

    loop(1, ZN, direct_sum)
    gather_z_end(pg, pz_s, pz_r)

    @pl.when(r != c)
    def _():
        remote(mfin.at[0], mfin.at[1], mp_s, mp_r, turned).wait_recv()

    grad = factor_grad[...].reshape(2 * R, TILE).astype(F32)
    rounded = (grad - dtot[...] - mfin[1].astype(F32)).astype(BF16)
    wide = rounded.astype(F32)

    none = jnp.zeros_like(wide)
    odd = rem(c, 2)
    padded = jnp.concatenate(
        [jnp.where(odd == 0, wide, none), jnp.where(odd == 0, none, wide)], axis=0
    )
    tslice[...] = padded.T.astype(BF16).reshape(N, R, 128)
    trecv[c] = tslice[c]

    def spread(d):
        k = rem(c + d, N)
        remote(tslice.at[k], trecv.at[c], tz_s.at[d], tz_r.at[c], z_dev(k)).start()

    loop(1, N, spread)

    dims = (((1,), (1,)), ((), ()))
    y0 = lax.dot_general(rounded, inverse[0], dims, preferred_element_type=F32)
    y1 = lax.dot_general(rounded, inverse[1], dims, preferred_element_type=F32)
    adjoint[...] = jnp.where(row_super == 0, y0, y1).astype(BF16).reshape(2, R, TILE)

    def wait_slice(d):
        k = rem(c + d, N)
        remote(trecv.at[k], trecv.at[k], tz_s.at[d], tz_r.at[k], z_dev(k)).wait_recv()

    loop(1, N, wait_slice)

    lane_tile = rem(lax.broadcasted_iota(jnp.int32, (R, 128), 1), 2 * R) // R
    lane_super = jnp.where(lane_tile == 0, s_row[0], s_row[1])
    blocks = []
    for q in range(N // 2):
        both = trecv[2 * q].astype(F32) + trecv[2 * q + 1].astype(F32)
        zero = jnp.zeros_like(both)
        blocks.append(
            jnp.concatenate(
                [jnp.where(lane_super == 0, both, zero), jnp.where(lane_super == 0, zero, both)], axis=0
            ).astype(BF16)
        )
    left = jnp.concatenate(blocks, axis=1)
    slab = jnp.dot(left, pg[...].reshape(2 * TILE, TILE), preferred_element_type=F32)
    for p in range(N):
        g, h = p // 2, p % 2
        rpart[p] = slab[8 * g:8 * g + 8, 256 * h:256 * h + 256]

    def reduce_x(d):
        p = rem(r + d, N)
        remote(rpart.at[p], rrecv.at[r], rx_s.at[d], rx_r.at[r], x_dev(p)).start()

    loop(1, N, reduce_x)
    rrecv[r] = rpart[r]

    def wait_reduce(d):
        p = rem(r + d, N)
        remote(rrecv.at[p], rrecv.at[p], rx_s.at[d], rx_r.at[p], x_dev(p)).wait_recv()

    loop(1, N, wait_reduce)
    done = rrecv[0]
    for p in range(1, N):
        done = done + rrecv[p]
    gz[c] = done * (1.0 / 128.0)

    half = div(c, ZN)

    def collect(d):
        k = index_at(rem(z + d, ZN), half)

        @pl.when(k != c)
        def _():
            remote(gz.at[c], gz.at[c], gz_s.at[d], gz_r.at[c], z_dev(k)).start()

    loop(0, ZN, collect)

    def wait_collect(d):
        k = core * ZN + d

        @pl.when(k != c)
        def _():
            remote(gz.at[k], gz.at[k], gz_s.at[d], gz_r.at[k], z_dev(k)).wait_recv()

    loop(0, ZN, wait_collect)
    own = gz[pl.ds(core * ZN, ZN)].reshape(8 * ZN, 256).astype(BF16)
    gx[r, core] = own

    def spread_x(d):
        remote(gx.at[r, core], gx.at[r, core], gx_s.at[d], gx_r.at[r, core], x_dev(rem(r + d, N))).start()

    loop(1, N, spread_x)
    remote(gx.at[r, core], gx.at[r, core], gx_s.at[0], gx_r.at[r, core], sib).start()

    def pass_x(d):
        p = rem(r + N - d, N)
        copy = remote(gx.at[p, core], gx.at[p, core], gx_s.at[N - 1 + d], gx_r.at[p, core], sib)
        copy.wait_recv()
        copy.start()

    loop(1, N, pass_x)

    def wait_pass(d):
        p = rem(r + N - d, N)
        remote(gx.at[p, 1 - core], gx.at[p, 1 - core], gx_s.at[0], gx_r.at[p, 1 - core], sib).wait_recv()

    loop(0, N, wait_pass)

    for p in range(N):
        g, h = p // 2, p % 2
        for a in range(2):
            inv_out[g // 4, a * ZN:(a + 1) * ZN, g % 4, :, 256 * h:256 * h + 256] = (
                gx[p, a].astype(F32).reshape(ZN, 8, 256)
            )

    @pl.when(r != c)
    def _():
        remote(frow.at[c], fcol.at[r], perm_s, perm_r, turned).wait_send()
        remote(mfin.at[0], mfin.at[1], mp_s, mp_r, turned).wait_send()

    def drain_x(d):
        remote(fcol.at[r], fcol.at[r], fx_s.at[d], fx_r.at[r], sib).wait_send()
        remote(mpart.at[r], mrecv.at[r], mx_s.at[d], mx_r.at[r], sib).wait_send()
        remote(tslice.at[c], trecv.at[c], tz_s.at[d], tz_r.at[c], sib).wait_send()
        remote(rpart.at[r], rrecv.at[r], rx_s.at[d], rx_r.at[r], sib).wait_send()

    loop(1, N, drain_x)

    def drain_z(d):
        remote(dpart.at[c], dsib.at[c], ds_s.at[d], ds_r.at[c], sib).wait_send()

        @pl.when(d < ZN - 1)
        def _():
            remote(dsum.at[c], drecv.at[c], dz_s.at[d], dz_r.at[c], sib).wait_send()

        @pl.when(index_at(rem(z + d, ZN), half) != c)
        def _():
            remote(gz.at[c], gz.at[c], gz_s.at[d], gz_r.at[c], sib).wait_send()

    loop(0, ZN, drain_z)

    def drain_g(d):
        remote(gx.at[r, core], gx.at[r, core], gx_s.at[d], gx_r.at[r, core], sib).wait_send()

    loop(0, 2 * N - 1, drain_g)


def local(panel, inverse, trail_grad, factor_grad, present, supernode):
    vmem = pl.BlockSpec(memory_space=pltpu.VMEM)
    smem = pl.BlockSpec(memory_space=pltpu.SMEM)
    dma = pltpu.SemaphoreType.DMA
    pieces = pltpu.VMEM((N, 2 * R, TILE), BF16)
    adjoint, spread = pl.pallas_call(
        kernel,
        out_shape=(
            jax.ShapeDtypeStruct((2, R, TILE), BF16),
            jax.ShapeDtypeStruct((2, N, 4, 8, TILE), F32),
        ),
        in_specs=[vmem, vmem, pl.BlockSpec(memory_space=pl.ANY), vmem, smem, smem],
        out_specs=(vmem, vmem),
        scratch_shapes=[
            pltpu.VMEM((2, 2, TILE, TILE), BF16),
            pltpu.VMEM((2, 2, TILE, TILE), BF16),
            pieces, pieces, pieces,
            pieces, pieces, pieces, pieces,
            pltpu.VMEM((2 * R, TILE), F32),
            pieces, pieces,
            pltpu.VMEM((2 * R, TILE), F32),
            pltpu.VMEM((2, 2 * R, TILE), BF16),
            pltpu.VMEM((N, R, 128), BF16),
            pltpu.VMEM((N, R, 128), BF16),
            pltpu.VMEM((N, 8, 256), F32),
            pltpu.VMEM((N, 8, 256), F32),
            pltpu.VMEM((N, 8, 256), F32),
            pltpu.VMEM((N, 2, 64, 256), BF16),
            dma,
            dma((15,)), dma((N,)), dma((15,)), dma((N,)),
            dma, dma,
            dma((N,)), dma((N,)),
            dma((ZN,)), dma((N,)), dma((ZN,)), dma((N,)),
            dma((N,)), dma((N,)),
            dma, dma,
            dma((N,)), dma((N,)),
            dma((N,)), dma((N,)),
            dma((ZN,)), dma((N,)),
            dma((31,)), dma((N, 2)),
        ],
        compiler_params=pltpu.CompilerParams(collective_id=0, has_side_effects=True),
    )(panel, inverse, trail_grad, factor_grad, present, supernode)
    inverse_adjoint = jnp.swapaxes(spread.reshape(2, TILE, TILE), 1, 2)
    return adjoint, inverse_adjoint


def solution(mesh):
    assert dict(mesh.shape) == {"row": N, "col": 8, "band": 2}
    in_specs = (
        P("row", ("col", "band"), None),
        P(),
        P("row", ("col", "band"), None, None),
        P("row", ("col", "band"), None),
        P("row", ("col", "band")),
        P(),
    )
    out_specs = (P("row", ("col", "band"), None), P())
    return jax.shard_map(local, mesh=mesh, in_specs=in_specs, out_specs=out_specs, check_vma=False)
```
